256 devices in a mesh: expert: 64 (over x, z, core), half: 4 (over y).
Axes of the slice: x: 4, y: 4, z: 8, core: 2. Of those that a mesh axis runs over, the one named last changes fastest.
Arguments:
- tokens: bfloat16 [2048, 4096], P('expert'), may hold values from -6 to 6
- target: bfloat16 [2048, 4096], P('expert', 'half'), may hold values from -3 to 3
- routes: int32 [2048, 8], P('expert'), may hold values from 0 to 63, all different within a row; in each aligned block of 32 rows (0 to 31, 32 to 63, ...) at most 8 rows name the same one
- route_scores: float32 [2048, 8], P('expert'), may hold values from 0.1 to 1
- in_codes: bfloat16 [64, 2, 4096, 1536], P('expert', None, None, 'half'), may hold values from 0 to 255, as said below
- in_low: float32 [64, 2, 32, 1536], P('expert', None, None, 'half'), may hold values from -0.0390625 to -0.015625
- in_high: float32 [64, 2, 32, 1536], P('expert', None, None, 'half'), may hold values from 0.015625 to 0.0390625
- down_codes: bfloat16 [64, 1536, 4096], P('expert', None, 'half'), may hold values from 0 to 255, as said below
- down_low: float32 [64, 12, 4096], P('expert', None, 'half'), may hold values from -0.063788794 to -0.02551552
- down_high: float32 [64, 12, 4096], P('expert', None, 'half'), may hold values from 0.02551552 to 0.063788794
Outputs:
- grad_tokens: bfloat16 [2048, 4096], P('expert', 'half')
- in_range_grad: float32 [64, 4, 32, 1536], P('expert', None, None, 'half')
- down_range_grad: float32 [64, 2, 12, 4096], P('expert', None, None, 'half')
The draws below stay inside these ranges and needn't reach their ends.
Inputs may be any that keep to these rules, and one draw needn't show every extreme that they name: `routes`: each row names 8 different experts. In each aligned block of 32 rows (the tokens of one index of expert) no expert is named by more than 8 rows, a bound that some block reaches. `in_codes`: whole numbers. `down_codes`: whole numbers.
All inputs are finite; a program needn't handle non-finite values.
Results may differ from the reference program's by a relative error of at most 0.013.
Values may be sent and summed in bfloat16 or wider, within the bound.
A program may use at most 128 MiB of HBM per device.

```python
import math
import jax
import jax.numpy as jnp
import numpy as np
from jax import lax

D = 4096
FF = 1536
TOP = 8
TOK_DEV = 32
EXPERTS = 64
CAP = 8
TOKENS = 2048
GD = 32
GF = 12
N_HALF = 4


def draw_in_codes(key, part):
    return jax.random.randint(key, (EXPERTS, 2, D, FF), 0, 256).astype(jnp.float32).astype(jnp.bfloat16)


def draw_down_codes(key, part):
    return jax.random.randint(key, (EXPERTS, FF, D), 0, 256).astype(jnp.float32).astype(jnp.bfloat16)


def block_levels(key, extent, split, smallest, high):
    level, own = 1.0, jax.random.fold_in(key, 6)
    for dim, shards_of in split:
        draws = jnp.exp(jax.random.uniform(jax.random.fold_in(own, dim), (shards_of,), jnp.float32, smallest / len(split), high / len(split)))
        level = level * jnp.repeat(draws, extent[dim] // shards_of).reshape([-1 if axis == dim else 1 for axis in range(len(extent))])
    return level


def assign_block(own_key, own, number, rows, number_of, top, limit, lean):
    order = jax.random.permutation(own_key, number_of)
    packed, common = shares(number_of, rows * top, limit, lean, True), shares(number_of, rows * top, limit, lean, False)
    places = jnp.arange(number_of)

    def named(lengths, offset_by):
        used = int((lengths > 0).sum())
        fixed = max(1, used // 4)
        passed = fixed + (places - fixed + offset_by * (used - fixed)) % max(1, number_of - fixed)
        return jnp.zeros((number_of,), jnp.int32).at[order[jnp.where(places < fixed, places, passed)]].set(jnp.asarray(lengths, jnp.int32))

    lengths = jnp.where(number % 4 == 0, named(packed, number // 4), named(common, number - number // 4 - 1))
    mixed = jax.random.permutation(jax.random.fold_in(own, 3), number_of)
    source_of, sink = mixed[0:number_of // 2 * 2:2], mixed[1:number_of // 2 * 2:2]
    room = jnp.minimum(lengths[source_of] - 1, limit - lengths[sink]) // 2
    room = jnp.where((source_of == order[0]) | (sink == order[0]) | (lengths[sink] == 0), 0, jnp.maximum(room, 0))
    passed = jax.random.randint(jax.random.fold_in(own, 4), (number_of // 2,), 0, 1 << 20) % (room + 1)
    lengths = lengths.at[source_of].add(-passed).at[sink].add(passed)
    items = jnp.searchsorted(jnp.cumsum(lengths), jnp.arange(rows * top), side="right").astype(jnp.int32)
    listing = items.reshape(top, rows).T
    listing = listing[jax.random.permutation(jax.random.fold_in(own, 1), rows)]
    offset_by = jax.random.randint(jax.random.fold_in(own, 2), (rows, 1), 0, top)
    return jnp.take_along_axis(listing, (jnp.arange(top)[None, :] + offset_by) % top, axis=1)


def shares(number_of, total, limit, lean, full):
    portions = [(1 << 20) // math.isqrt(standing ** lean) + 1 for standing in range(1, number_of + 1)]
    largest = limit if full else min(limit, max(-(-total // number_of), total * portions[0] // sum(portions)))
    least = 1 if total - largest >= number_of - 1 else 0
    given, rest = [largest] + [least] * (number_of - 1), total - largest - least * (number_of - 1)
    while rest > 0:
        candidates = [i for i in range(1, number_of) if given[i] < largest] or [i for i in range(1, number_of) if given[i] < limit]
        pool, left = sum([portions[i] for i in candidates]), rest
        for i in candidates:
            extra = min(limit - given[i], max(1, left * portions[i] // pool), rest)
            given[i] = given[i] + extra
            rest = rest - extra
    return np.array(given)


def centred(stream_key, dims, scale, reach, shards=(), held_as=jnp.bfloat16):
    gain = block_levels(stream_key, dims, shards, -0.22, 0.18) if shards else 1.0
    array = jax.random.normal(stream_key, dims, jnp.float32) * scale * gain
    return jnp.minimum(jnp.maximum(array, -reach), reach).astype(held_as)


def setup_inputs(seed: int = 0) -> dict:
    streams_of = jax.random.split(jax.random.key(seed), 11)
    tokens = centred(streams_of[0], (TOKENS, D), 1.0, 6.0, ((0, 64),))
    target = centred(streams_of[1], (TOKENS, D), 0.5, 3.0, ((0, 64), (1, 4)))
    routes_keys = jax.random.split(jax.random.fold_in(streams_of[2], 1), TOKENS // TOK_DEV)
    routes_turns = jax.random.permutation(jax.random.fold_in(streams_of[2], 3), TOKENS // TOK_DEV)
    routes = jax.vmap(lambda own, number: assign_block(jax.random.fold_in(streams_of[2], 2), own, number, TOK_DEV, EXPERTS, TOP, CAP, 2))(routes_keys, routes_turns).reshape((TOKENS, TOP))
    route_scores = jnp.clip(jnp.exp(math.log(1.0) - 2.3025851 * jax.random.uniform(streams_of[3], (TOKENS, TOP), jnp.float32) ** block_levels(streams_of[3], (TOKENS, TOP), ((0, 64),), -0.2, 0.2)), 0.1, 1.0)
    in_codes = draw_in_codes(jax.random.fold_in(streams_of[10], 71), 0)
    in_low = jnp.clip(-0.0390625 + 0.0234375 * jax.random.uniform(streams_of[5], (EXPERTS, 2, GD, FF), jnp.float32) ** block_levels(streams_of[5], (EXPERTS, 2, GD, FF), ((0, 64), (3, 4)), -0.2, 0.2), -0.0390625, -0.015625)
    in_high = jnp.clip(0.015625 + 0.0234375 * jax.random.uniform(streams_of[6], (EXPERTS, 2, GD, FF), jnp.float32) ** block_levels(streams_of[6], (EXPERTS, 2, GD, FF), ((0, 64), (3, 4)), -0.2, 0.2), 0.015625, 0.0390625)
    down_codes = draw_down_codes(jax.random.fold_in(streams_of[10], 71), 0)
    down_low = jnp.clip(-0.063788794 + 0.038273275 * jax.random.uniform(streams_of[8], (EXPERTS, GF, D), jnp.float32) ** block_levels(streams_of[8], (EXPERTS, GF, D), ((0, 64), (2, 4)), -0.2, 0.2), -0.063788794, -0.02551552)
    down_high = jnp.clip(0.02551552 + 0.038273275 * jax.random.uniform(streams_of[9], (EXPERTS, GF, D), jnp.float32) ** block_levels(streams_of[9], (EXPERTS, GF, D), ((0, 64), (2, 4)), -0.2, 0.2), 0.02551552, 0.063788794)
    return {"tokens": tokens, "target": target, "routes": routes, "route_scores": route_scores, "in_codes": in_codes, "in_low": in_low, "in_high": in_high, "down_codes": down_codes, "down_low": down_low, "down_high": down_high}


def route_tables(route_block, experts, capacity):
    flat_ids = route_block.reshape(-1).astype(jnp.int32)
    pair_count = flat_ids.shape[0]
    onehot = (flat_ids[:, None] == jnp.arange(experts, dtype=jnp.int32)[None, :]).astype(jnp.int32)
    before = (jnp.cumsum(onehot, axis=0) - onehot).astype(jnp.int32)
    slot_rank = jnp.sum(before * onehot, axis=1).astype(jnp.int32)
    dest_slot = (flat_ids * capacity + slot_rank).astype(jnp.int32)
    matches = dest_slot[None, :] == jnp.arange(experts * capacity, dtype=jnp.int32)[:, None]
    is_valid = jnp.any(matches, axis=1)
    source = jnp.sum(jnp.where(matches, jnp.arange(pair_count, dtype=jnp.int32)[None, :], 0), axis=1).astype(jnp.int32)
    return dest_slot, source, is_valid


def dequant(code_vals, low_edge, high_edge):
    groups = low_edge.shape[0]
    scaled = code_vals.astype(jnp.float32).reshape(groups, -1, code_vals.shape[-1]) / 255.0
    weight = low_edge[:, None, :] + (high_edge - low_edge)[:, None, :] * scaled
    return weight.reshape(code_vals.shape).astype(jnp.bfloat16)


def range_grads(grad_weight, code_vals, groups):
    shaped = grad_weight.reshape(groups, -1, grad_weight.shape[-1])
    scaled = code_vals.astype(jnp.float32).reshape(groups, -1, code_vals.shape[-1]) / 255.0
    low_grad = jnp.sum(shaped * (1.0 - scaled), axis=1)
    high_grad = jnp.sum(shaped * scaled, axis=1)
    return low_grad, high_grad


def contract_rows(left, right):
    return lax.dot_general(left, right, (((0,), (0,)), ((), ())), preferred_element_type=jnp.float32)


def contract_cols(left, right):
    return lax.dot_general(left, right, (((1,), (1,)), ((), ())), preferred_element_type=jnp.float32)


def reference(tokens, target, routes, route_scores, in_codes, in_low, in_high, down_codes, down_low, down_high):
    experts = in_codes.shape[0]
    sources = routes.shape[0] // TOK_DEV
    pairs = TOK_DEV * TOP
    blocks = routes.reshape(sources, TOK_DEV, TOP).astype(jnp.int32)
    dest_slot, source, is_valid = jax.vmap(lambda block_ids: route_tables(block_ids, experts, CAP))(blocks)
    weights = route_scores / jnp.sum(route_scores, axis=1, keepdims=True)
    base = jnp.arange(sources, dtype=jnp.int32)[:, None]
    token_index = (base * TOK_DEV + source // TOP).astype(jnp.int32)
    pair_index = (base * pairs + source).astype(jnp.int32)

    def by_expert(table):
        return table.reshape(sources, experts, CAP).transpose(1, 0, 2).reshape(experts, sources * CAP)

    token_index = by_expert(token_index)
    pair_index = by_expert(pair_index)
    row_live = by_expert(is_valid)

    def expert_forward(expert_item):
        code_vals, low_edge, high_edge, down_vals, down_low_edge, down_high_edge, row_index, live_rows = expert_item
        w_gate = dequant(code_vals[0], low_edge[0], high_edge[0])
        w_up = dequant(code_vals[1], low_edge[1], high_edge[1])
        w_down = dequant(down_vals, down_low_edge, down_high_edge)
        expert_rows = jnp.where(live_rows[:, None], tokens[row_index], jnp.zeros((), tokens.dtype))
        gate_pre = jnp.dot(expert_rows, w_gate, preferred_element_type=jnp.float32)
        up_pre = jnp.dot(expert_rows, w_up, preferred_element_type=jnp.float32)
        sigmoid_gate = jax.nn.sigmoid(gate_pre)
        hidden = (gate_pre * sigmoid_gate * up_pre).astype(jnp.bfloat16)
        return jnp.dot(hidden, w_down, preferred_element_type=jnp.float32).astype(jnp.bfloat16)

    outputs = lax.map(expert_forward, (in_codes, in_low, in_high, down_codes, down_low, down_high, token_index, row_live))
    slot_rank = (dest_slot % CAP).reshape(sources, TOK_DEV, TOP).astype(jnp.int32)
    source_ids = jnp.broadcast_to(base[:, :, None], (sources, TOK_DEV, TOP))
    picked = outputs.reshape(experts, sources, CAP, -1)[blocks, source_ids, slot_rank]
    picked = picked.reshape(sources * TOK_DEV, TOP, -1).astype(jnp.float32)
    mixed_out = jnp.sum(weights[:, :, None] * picked, axis=1)
    recon_error = mixed_out - target.astype(jnp.float32)
    error_grads = (weights[:, :, None] * recon_error[:, None, :]).astype(jnp.bfloat16).reshape(sources * pairs, -1)

    def expert_backward(expert_item):
        code_vals, low_edge, high_edge, down_vals, down_low_edge, down_high_edge, row_index, err_index, live_rows = expert_item
        w_gate = dequant(code_vals[0], low_edge[0], high_edge[0])
        w_up = dequant(code_vals[1], low_edge[1], high_edge[1])
        w_down = dequant(down_vals, down_low_edge, down_high_edge)
        expert_rows = jnp.where(live_rows[:, None], tokens[row_index], jnp.zeros((), tokens.dtype))
        grad_in = jnp.where(live_rows[:, None], error_grads[err_index], jnp.zeros((), error_grads.dtype))
        gate_pre = jnp.dot(expert_rows, w_gate, preferred_element_type=jnp.float32)
        up_pre = jnp.dot(expert_rows, w_up, preferred_element_type=jnp.float32)
        sigmoid_gate = jax.nn.sigmoid(gate_pre)
        gate_act = gate_pre * sigmoid_gate
        hidden = (gate_act * up_pre).astype(jnp.bfloat16)
        grad_hidden = contract_cols(grad_in, w_down)
        grad_gate = (grad_hidden * up_pre * sigmoid_gate * (1.0 + gate_pre * (1.0 - sigmoid_gate))).astype(jnp.bfloat16)
        grad_up = (grad_hidden * gate_act).astype(jnp.bfloat16)
        gate_low, gate_high = range_grads(contract_rows(expert_rows, grad_gate), code_vals[0], low_edge.shape[1])
        up_low, up_high = range_grads(contract_rows(expert_rows, grad_up), code_vals[1], low_edge.shape[1])
        down_lowg, down_highg = range_grads(contract_rows(hidden, grad_in), down_vals, down_low_edge.shape[0])
        quarter_ff = grad_gate.shape[1] // N_HALF
        row_total = jnp.zeros((grad_gate.shape[0], w_gate.shape[0]), jnp.float32)
        for quarter in range(N_HALF):
            start = quarter * quarter_ff
            stop = start + quarter_ff
            row_part = (contract_cols(grad_gate[:, start:stop], w_gate[:, start:stop]) + contract_cols(grad_up[:, start:stop], w_up[:, start:stop])).astype(jnp.bfloat16)
            row_part = lax.optimization_barrier(row_part)
            row_total = row_total + row_part.astype(jnp.float32)
        grad_rows = row_total.astype(jnp.bfloat16)
        return jnp.stack([gate_low, gate_high, up_low, up_high]), jnp.stack([down_lowg, down_highg]), grad_rows

    in_grad, down_grad, grad_rows = lax.map(expert_backward, (in_codes, in_low, in_high, down_codes, down_low, down_high, token_index, pair_index, row_live))
    grad_picked = grad_rows.reshape(experts, sources, CAP, -1)[blocks, source_ids, slot_rank]
    grad_picked = grad_picked.reshape(sources * TOK_DEV, TOP, -1).astype(jnp.float32)
    grad_tokens = jnp.sum(grad_picked, axis=1).astype(jnp.bfloat16)
    return grad_tokens, in_grad, down_grad
```

```python
import functools

import jax
import jax.numpy as jnp
from jax import lax
from jax.experimental import pallas as pl
from jax.experimental.pallas import tpu as pltpu
from jax.sharding import PartitionSpec as P

EX, EZ, CORES, HALVES = 4, 8, 2, 4
MESH = pl.DeviceIdType.MESH


def ring(base, step, size):
    return lax.rem(base + step + 2 * size, size)


def plane_tree():
    up, order = {}, []
    seen = [(0, 0, 0), (1, 0, 0)]
    while seen:
        order += seen
        later = []
        for h, dx, dz in seen:
            steps = []
            z_first = h == 0
            if dx == 0 or not z_first:
                if 0 <= dz < EZ // 2:
                    steps.append((dx, dz + 1, "zf"))
                if -(EZ // 2 - 1) < dz <= 0:
                    steps.append((dx, dz - 1, "zb"))
            if dz == 0 or z_first:
                if 0 <= dx < EX // 2:
                    steps.append((dx + 1, dz, "xf"))
                if -(EX // 2 - 1) < dx <= 0:
                    steps.append((dx - 1, dz, "xb"))
            for nx, nz, way in steps:
                up[(h, nx, nz)] = ((h, dx, dz), way)
                later.append((h, nx, nz))
        seen = later
    down = {piece: [] for piece in order}
    for piece, (parent, way) in up.items():
        down[parent].append((piece, way))
    return order, up, down


BACK = {"xf": "xb", "xb": "xf", "zf": "zb", "zb": "zf"}


class Plane:
    def __init__(self):
        e = lax.axis_index("expert")
        self.c = e % CORES
        self.z = (e // CORES) % EZ
        self.x = e // (CORES * EZ)
        self.sign = 1 - 2 * self.c
        self.order, self.up, self.down = plane_tree()
        self.index = {piece: i for i, piece in enumerate(self.order)}

    def at(self, dx, dz, core):
        x = ring(self.x, self.sign * dx, EX)
        z = ring(self.z, self.sign * dz, EZ)
        return (x * EZ + z) * CORES + core

    def near(self, way):
        step = 1 if way[1] == "f" else -1
        return {"expert": self.at(step, 0, self.c) if way[0] == "x" else self.at(0, step, self.c)}

    def partner(self):
        return {"expert": self.at(0, 0, 1 - self.c)}

    def greet(self):
        barrier = pltpu.get_barrier_semaphore()
        for device in [self.near(way) for way in BACK] + [self.partner()]:
            pl.semaphore_signal(barrier, inc=1, device_id=device, device_id_type=MESH)
        pl.semaphore_wait(barrier, 5)


def plane_gather_kernel(x_ref, out_ref, send, recv, psend, precv, own):
    plane = Plane()
    rows = x_ref.shape[0]
    part = rows // 2
    plane.greet()

    def place(block, h):
        return out_ref.at[pl.ds(pl.multiple_of(block * rows + h * part, part), part), :]

    def held(piece):
        h, dx, dz = piece
        if dx == 0 and dz == 0:
            return x_ref.at[pl.ds(h * part, part), :]
        return place(plane.at(-dx, -dz, plane.c), h)

    def hop(piece, way):
        h, dx, dz = piece
        parent, _ = plane.up[piece]
        source = plane.at(-parent[1], -parent[2], plane.c)
        i = plane.index[piece]
        return pltpu.make_async_remote_copy(
            src_ref=held(parent), dst_ref=place(source, h), send_sem=send.at[i],
            recv_sem=recv.at[i], device_id=plane.near(way), device_id_type=MESH)

    def arrival(piece):
        h, dx, dz = piece
        i = plane.index[piece]
        spot = place(plane.at(-dx, -dz, plane.c), h)
        return pltpu.make_async_remote_copy(
            src_ref=spot, dst_ref=spot, send_sem=send.at[i], recv_sem=recv.at[i],
            device_id=plane.partner(), device_id_type=MESH)

    def across(piece):
        h, dx, dz = piece
        i = plane.index[piece]
        return pltpu.make_async_remote_copy(
            src_ref=held(piece), dst_ref=place(plane.at(-dx, -dz, plane.c), h),
            send_sem=psend.at[i], recv_sem=precv.at[i],
            device_id=plane.partner(), device_id_type=MESH)

    def across_in(piece):
        h, dx, dz = piece
        i = plane.index[piece]
        spot = place(plane.at(dx, dz, 1 - plane.c), h)
        return pltpu.make_async_remote_copy(
            src_ref=spot, dst_ref=spot, send_sem=psend.at[i], recv_sem=precv.at[i],
            device_id=plane.partner(), device_id_type=MESH)

    mine = pltpu.make_async_copy(
        x_ref, out_ref.at[pl.ds(pl.multiple_of(plane.at(0, 0, plane.c) * rows, rows), rows), :], own)
    started = []
    for piece in plane.order:
        if piece in plane.up:
            arrival(piece).wait_recv()
        for child, way in plane.down[piece]:
            copy = hop(child, way)
            copy.start()
            started.append(copy)
        copy = across(piece)
        copy.start()
        started.append(copy)
    mine.start()
    for piece in plane.order:
        across_in(piece).wait_recv()
    mine.wait()
    for copy in started:
        copy.wait_send()


def plane_gather(x, cid):
    rows, cols = x.shape
    n = 2 * EX * EZ
    return pl.pallas_call(
        plane_gather_kernel,
        out_shape=jax.ShapeDtypeStruct((rows * EX * EZ * CORES, cols), x.dtype),
        in_specs=[pl.BlockSpec(memory_space=pltpu.VMEM)],
        out_specs=pl.BlockSpec(memory_space=pltpu.VMEM),
        scratch_shapes=[pltpu.SemaphoreType.DMA((n,))] * 4 + [pltpu.SemaphoreType.DMA],
        compiler_params=pltpu.CompilerParams(collective_id=cid, has_side_effects=True),
        name=f"plane_gather_{cid}",
    )(x)


def plane_reduce_kernel(d_ref, out_ref, other, total, inbox, send, recv, psend, precv):
    plane = Plane()
    rows = out_ref.shape[0]
    part = rows // 2
    plane.greet()

    def mine(block, h):
        return d_ref.at[pl.ds(pl.multiple_of(block * rows + h * part, part), part), :]

    def across(piece):
        h, dx, dz = piece
        i = plane.index[piece]
        return pltpu.make_async_remote_copy(
            src_ref=mine(plane.at(dx, dz, 1 - plane.c), h), dst_ref=other.at[i],
            send_sem=psend.at[i], recv_sem=precv.at[i],
            device_id=plane.partner(), device_id_type=MESH)

    order = plane.order[::-1]
    for piece in order:
        across(piece).start()
    for piece in order:
        h, dx, dz = piece
        i = plane.index[piece]
        across(piece).wait_recv()
        value = mine(plane.at(-dx, -dz, plane.c), h)[...].astype(jnp.float32)
        value = value + other[i].astype(jnp.float32)
        for child, way in plane.down[piece]:
            j = plane.index[child]
            pltpu.make_async_remote_copy(
                src_ref=total.at[j], dst_ref=inbox.at[j], send_sem=send.at[j],
                recv_sem=recv.at[j], device_id=plane.partner(), device_id_type=MESH).wait_recv()
            value = value + inbox[j].astype(jnp.float32)
        if piece in plane.up:
            total[i] = value.astype(total.dtype)
            pltpu.make_async_remote_copy(
                src_ref=total.at[i], dst_ref=inbox.at[i], send_sem=send.at[i],
                recv_sem=recv.at[i], device_id=plane.near(BACK[plane.up[piece][1]]),
                device_id_type=MESH).start()
        else:
            out_ref[pl.ds(h * part, part), :] = value
    for piece in order:
        i = plane.index[piece]
        across(piece).wait_send()
        if piece in plane.up:
            pltpu.make_async_remote_copy(
                src_ref=total.at[i], dst_ref=inbox.at[i], send_sem=send.at[i],
                recv_sem=recv.at[i], device_id=plane.partner(), device_id_type=MESH).wait_send()


def plane_reduce(d, cid):
    rows, cols = d.shape[0] // (EX * EZ * CORES), d.shape[1]
    n = 2 * EX * EZ
    return pl.pallas_call(
        plane_reduce_kernel,
        out_shape=jax.ShapeDtypeStruct((rows, cols), jnp.float32),
        in_specs=[pl.BlockSpec(memory_space=pltpu.VMEM)],
        out_specs=pl.BlockSpec(memory_space=pltpu.VMEM),
        scratch_shapes=[pltpu.VMEM((n, rows // 2, cols), d.dtype)] * 3
        + [pltpu.SemaphoreType.DMA((n,))] * 4,
        compiler_params=pltpu.CompilerParams(collective_id=cid, has_side_effects=True),
        name=f"plane_reduce_{cid}",
    )(d)


class Column:
    def __init__(self):
        self.y = lax.axis_index("half")

    def at(self, step):
        return ring(self.y, step, HALVES)

    def near(self, step):
        return {"half": self.at(step)}

    def greet(self):
        barrier = pltpu.get_barrier_semaphore()
        for step in (1, -1):
            pl.semaphore_signal(barrier, inc=1, device_id=self.near(step), device_id_type=MESH)
        pl.semaphore_wait(barrier, 2)


NEAR = [(0, 1), (1, -1), (1, 1), (0, -1)]


def column_gather_kernel(x_ref, out_ref, send, recv, own):
    col = Column()
    rows, cols = x_ref.shape
    part = rows // 2
    col.greet()

    def place(source, h):
        return out_ref.at[pl.ds(h * part, part), pl.ds(pl.multiple_of(source * cols, 128), cols)]

    def copy(i, src, source, h, step):
        return pltpu.make_async_remote_copy(
            src_ref=src, dst_ref=place(source, h), send_sem=send.at[i], recv_sem=recv.at[i],
            device_id=col.near(step), device_id_type=MESH)

    started = []
    for i, (h, step) in enumerate(NEAR):
        started.append(copy(i, x_ref.at[pl.ds(h * part, part), :], col.y, h, step))
    mine = pltpu.make_async_copy(
        x_ref, out_ref.at[:, pl.ds(pl.multiple_of(col.y * cols, 128), cols)], own)
    for c in started:
        c.start()
    mine.start()
    for i, (h, step) in enumerate(NEAR):
        source = col.at(-step)
        copy(i, place(source, h), source, h, step).wait_recv()
        if i < 2:
            c = copy(4 + i, place(source, h), source, h, step)
            c.start()
            started.append(c)
    for i, (h, step) in enumerate(NEAR[:2]):
        source = col.at(2)
        copy(4 + i, place(source, h), source, h, step).wait_recv()
    mine.wait()
    for c in started:
        c.wait_send()


def column_gather(x, cid):
    rows, cols = x.shape
    return pl.pallas_call(
        column_gather_kernel,
        out_shape=jax.ShapeDtypeStruct((rows, cols * HALVES), x.dtype),
        in_specs=[pl.BlockSpec(memory_space=pltpu.VMEM)],
        out_specs=pl.BlockSpec(memory_space=pltpu.VMEM),
        scratch_shapes=[pltpu.SemaphoreType.DMA((6,))] * 2 + [pltpu.SemaphoreType.DMA],
        compiler_params=pltpu.CompilerParams(collective_id=cid, has_side_effects=True),
        name=f"column_gather_{cid}",
    )(x)


def column_reduce_kernel(d_ref, out_ref, inbox, total, send, recv):
    col = Column()
    rows, cols = out_ref.shape
    part = rows // 2
    tile = 32
    col.greet()

    def mine(dest, start, size):
        return d_ref.at[pl.ds(start, size), pl.ds(pl.multiple_of(dest * cols, 128), cols)]

    def copy(i, src, step):
        return pltpu.make_async_remote_copy(
            src_ref=src, dst_ref=inbox.at[i], send_sem=send.at[i], recv_sem=recv.at[i],
            device_id=col.near(step), device_id_type=MESH)

    started = []
    for i, (h, step) in enumerate(NEAR[:2]):
        started.append(copy(4 + i, mine(col.at(2), h * part, part), -step))
    for i, (h, step) in enumerate(NEAR[2:]):
        started.append(copy(2 + i, mine(col.at(-step), h * part, part), -step))
    for c in started:
        c.start()
    for i, (h, step) in enumerate(NEAR[:2]):
        copy(4 + i, total.at[i], step).wait_recv()

        def join(t, carry, i=i, h=h, step=step):
            start = pl.multiple_of(t * tile, tile)
            a = mine(col.at(-step), pl.multiple_of(h * part + start, tile), tile)[...]
            b = inbox[4 + i, pl.ds(start, tile), :]
            total[i, pl.ds(start, tile), :] = (
                a.astype(jnp.float32) + b.astype(jnp.float32)).astype(total.dtype)
            return carry

        lax.fori_loop(0, part // tile, join, 0)
        c = copy(i, total.at[i], -step)
        c.start()
        started.append(c)
    for i in (2, 3, 0, 1):
        copy(i, total.at[0], 1).wait_recv()
    for h in (0, 1):
        a, b = [i for i in range(4) if NEAR[i][0] == h]

        def join(t, carry, a=a, b=b, h=h):
            start = pl.multiple_of(t * tile, tile)
            spot = pl.multiple_of(h * part + start, tile)
            value = mine(col.y, spot, tile)[...].astype(jnp.float32)
            value = value + inbox[a, pl.ds(start, tile), :].astype(jnp.float32)
            value = value + inbox[b, pl.ds(start, tile), :].astype(jnp.float32)
            out_ref[pl.ds(spot, tile), :] = value.astype(out_ref.dtype)
            return carry

        lax.fori_loop(0, part // tile, join, 0)
    for c in started:
        c.wait_send()


def column_reduce(d, cid, dtype):
    rows, cols = d.shape[0], d.shape[1] // HALVES
    return pl.pallas_call(
        column_reduce_kernel,
        out_shape=jax.ShapeDtypeStruct((rows, cols), dtype),
        in_specs=[pl.BlockSpec(memory_space=pltpu.VMEM)],
        out_specs=pl.BlockSpec(memory_space=pltpu.VMEM),
        scratch_shapes=[pltpu.VMEM((6, rows // 2, cols), d.dtype),
                        pltpu.VMEM((2, rows // 2, cols), d.dtype)]
        + [pltpu.SemaphoreType.DMA((6,))] * 2,
        compiler_params=pltpu.CompilerParams(collective_id=cid, has_side_effects=True),
        name=f"column_reduce_{cid}",
    )(d)


def dequant(code_vals, low_edge, high_edge):
    groups = low_edge.shape[0]
    scaled = code_vals.astype(jnp.float32).reshape(groups, -1, code_vals.shape[-1]) / 255.0
    weight = low_edge[:, None, :] + (high_edge - low_edge)[:, None, :] * scaled
    return weight.reshape(code_vals.shape).astype(jnp.bfloat16)


def range_grads(grad_weight, code_vals, groups):
    shaped = grad_weight.reshape(groups, -1, grad_weight.shape[-1])
    scaled = code_vals.astype(jnp.float32).reshape(groups, -1, code_vals.shape[-1]) / 255.0
    low_grad = jnp.sum(shaped * (1.0 - scaled), axis=1)
    high_grad = jnp.sum(shaped * scaled, axis=1)
    return (low_grad, high_grad)


def contract_rows(left, right):
    return lax.dot_general(
        left, right, (((0,), (0,)), ((), ())), preferred_element_type=jnp.float32
    )


def contract_cols(left, right):
    return lax.dot_general(
        left, right, (((1,), (1,)), ((), ())), preferred_element_type=jnp.float32
    )


def local(
    tokens, target, routes, route_scores, in_codes, in_low, in_high, down_codes, down_low, down_high
):
    bf16, f32 = jnp.bfloat16, jnp.float32
    experts = lax.axis_size("expert")
    expert = lax.axis_index("expert")
    tok_count, top_count = routes.shape
    quarter = target.shape[1]
    all_tokens = experts * tok_count
    slots = experts * min(tok_count, 2 * tok_count * top_count // experts)

    weights = route_scores / jnp.sum(route_scores, axis=1, keepdims=True)
    terms, rest = [routes.astype(bf16)], weights
    for _ in range(3):
        term = lax.reduce_precision(rest, 8, 7)
        terms.append(term.astype(bf16))
        rest = rest - term
    side = jnp.concatenate(terms, axis=1)
    side = jnp.pad(side, ((0, 0), (0, 128 - side.shape[1])))
    own = lax.dynamic_slice_in_dim(tokens, lax.axis_index("half") * quarter, quarter, 1)
    spread = plane_gather(jnp.concatenate([own, side], axis=1), 0)

    side = spread[:, quarter:quarter + 4 * top_count].astype(f32)
    named = side[:, :top_count] == expert.astype(f32)
    weight_of = sum(side[:, k * top_count:(k + 1) * top_count] for k in (1, 2, 3))
    weight_of = jnp.sum(jnp.where(named, weight_of, 0.0), axis=1)
    live = jnp.any(named, axis=1)
    rank = jnp.cumsum(live.astype(jnp.int32)) - 1
    picks = live[None, :] & (rank[None, :] == jnp.arange(slots, dtype=jnp.int32)[:, None])
    slot_weight = jnp.sum(jnp.where(picks, weight_of[None, :], 0.0), axis=1)
    picks = picks.astype(bf16)

    w_gate = dequant(in_codes[0, 0], in_low[0, 0], in_high[0, 0])
    w_up = dequant(in_codes[0, 1], in_low[0, 1], in_high[0, 1])
    w_down = dequant(down_codes[0], down_low[0], down_high[0])

    expert_rows = jnp.dot(picks, spread[:, :quarter], preferred_element_type=f32).astype(bf16)
    expert_rows = column_gather(expert_rows, 1)
    gate_pre = jnp.dot(expert_rows, w_gate, preferred_element_type=f32)
    up_pre = jnp.dot(expert_rows, w_up, preferred_element_type=f32)
    sigmoid_gate = jax.nn.sigmoid(gate_pre)
    gate_act = gate_pre * sigmoid_gate
    hidden = (gate_act * up_pre).astype(bf16)
    hidden_all = column_gather(hidden, 2)
    out_rows = jnp.dot(hidden_all, w_down, preferred_element_type=f32)
    out_rows = (out_rows * slot_weight[:, None]).astype(bf16)
    mixed_out = plane_reduce(contract_rows(picks, out_rows).astype(bf16), 3)
    recon_error = mixed_out - target.astype(f32)
    errors = plane_gather(recon_error.astype(bf16), 4)
    error_grads = jnp.dot(picks, errors, preferred_element_type=f32)
    error_grads = (error_grads * slot_weight[:, None]).astype(bf16)
    partial_hidden = contract_cols(error_grads, w_down).astype(bf16)
    grad_hidden = column_reduce(partial_hidden, 5, f32)
    grad_gate = (
        grad_hidden * up_pre * sigmoid_gate * (1.0 + gate_pre * (1.0 - sigmoid_gate))
    ).astype(bf16)
    grad_up = (grad_hidden * gate_act).astype(bf16)
    row_part = (contract_cols(grad_gate, w_gate) + contract_cols(grad_up, w_up)).astype(bf16)
    grad_rows = column_reduce(row_part, 6, bf16)
    grad_tokens = plane_reduce(contract_rows(picks, grad_rows).astype(bf16), 7).astype(bf16)

    groups_width = in_low.shape[2]
    gate_low, gate_high = range_grads(
        contract_rows(expert_rows, grad_gate), in_codes[0, 0], groups_width
    )
    up_low, up_high = range_grads(contract_rows(expert_rows, grad_up), in_codes[0, 1], groups_width)
    down_lowg, down_highg = range_grads(
        contract_rows(hidden_all, error_grads), down_codes[0], down_low.shape[1]
    )
    in_grad = jnp.stack([gate_low, gate_high, up_low, up_high])[None]
    down_grad = jnp.stack([down_lowg, down_highg])[None]
    return (grad_tokens, in_grad, down_grad)


def solution(mesh):
    placed = (
        P("expert", None),
        P("expert", "half"),
        P("expert", None),
        P("expert", None),
        P("expert", None, None, "half"),
        P("expert", None, None, "half"),
        P("expert", None, None, "half"),
        P("expert", None, "half"),
        P("expert", None, "half"),
        P("expert", None, "half"),
    )
    return jax.shard_map(
        local,
        mesh=mesh,
        in_specs=placed,
        out_specs=(
            P("expert", "half"),
            P("expert", None, None, "half"),
            P("expert", None, None, "half"),
        ),
        check_vma=False,
    )
```

```python
import functools

import jax
import jax.numpy as jnp
from jax import lax
from jax.experimental import pallas as pl
from jax.experimental.pallas import tpu as pltpu
from jax.sharding import PartitionSpec as P

EX, EZ, CORES, HALVES = 4, 8, 2, 4
MESH = pl.DeviceIdType.MESH


def ring(base, step, size):
    return lax.rem(base + step + 2 * size, size)


def plane_tree():
    up, order = {}, []
    seen = [(0, 0, 0), (1, 0, 0)]
    while seen:
        order += seen
        later = []
        for h, dx, dz in seen:
            steps = []
            z_first = h == 0
            if dx == 0 or not z_first:
                if 0 <= dz < EZ // 2:
                    steps.append((dx, dz + 1, "zf"))
                if -(EZ // 2 - 1) < dz <= 0:
                    steps.append((dx, dz - 1, "zb"))
            if dz == 0 or z_first:
                if 0 <= dx < EX // 2:
                    steps.append((dx + 1, dz, "xf"))
                if -(EX // 2 - 1) < dx <= 0:
                    steps.append((dx - 1, dz, "xb"))
            for nx, nz, way in steps:
                up[(h, nx, nz)] = ((h, dx, dz), way)
                later.append((h, nx, nz))
        seen = later
    down = {piece: [] for piece in order}
    for piece, (parent, way) in up.items():
        down[parent].append((piece, way))
    return order, up, down


BACK = {"xf": "xb", "xb": "xf", "zf": "zb", "zb": "zf"}


class Plane:
    def __init__(self):
        e = lax.axis_index("expert")
        self.expert = e
        self.c = e % CORES
        self.z = (e // CORES) % EZ
        self.x = e // (CORES * EZ)
        self.sign = 1 - 2 * self.c
        self.order, self.up, self.down = plane_tree()
        self.index = {piece: i for i, piece in enumerate(self.order)}

    def chip(self, dx, dz):
        return ring(self.x, self.sign * dx, EX) * EZ + ring(self.z, self.sign * dz, EZ)

    def at(self, dx, dz, core):
        return self.chip(dx, dz) * CORES + core

    def near(self, way):
        step = 1 if way[1] == "f" else -1
        return {"expert": self.at(step, 0, self.c) if way[0] == "x" else self.at(0, step, self.c)}

    def partner(self):
        return {"expert": self.at(0, 0, 1 - self.c)}

    def devices(self):
        return [self.near(way) for way in BACK] + [self.partner()]


def greet(devices):
    barrier = pltpu.get_barrier_semaphore()
    for device in devices:
        pl.semaphore_signal(barrier, inc=1, device_id=device, device_id_type=MESH)
    pl.semaphore_wait(barrier, len(devices))


def remote(src, dst, send, recv, device):
    return pltpu.make_async_remote_copy(
        src_ref=src, dst_ref=dst, send_sem=send, recv_sem=recv, device_id=device,
        device_id_type=MESH)


def split_of(cols):
    first = cols * 19 // 32 // 128 * 128
    return ((0, first), (first, cols - first)) if first else ((0, 128), (0, 128))


class Spread:
    def __init__(self, plane, x_ref, out, split, send, recv, psend, precv):
        self.p, self.x_ref, self.out, self.split = plane, x_ref, out, split
        self.send, self.recv, self.psend, self.precv = send, recv, psend, precv
        self.rows = x_ref.shape[0]
        self.started = []

    def place(self, block, h):
        start, size = self.split[h]
        rows = self.rows
        return self.out.at[pl.ds(pl.multiple_of(block * rows, rows), rows), pl.ds(start, size)]

    def held(self, piece):
        h, dx, dz = piece
        if dx == 0 and dz == 0:
            start, size = self.split[h]
            return self.x_ref.at[:, pl.ds(start, size)]
        return self.place(self.p.at(-dx, -dz, self.p.c), h)

    def forward(self, piece):
        p, (h, dx, dz) = self.p, piece
        i = p.index[piece]
        spot = self.place(p.at(-dx, -dz, p.c), h)
        if piece in p.up:
            remote(spot, spot, self.send.at[i], self.recv.at[i], p.partner()).wait_recv()
        copies = []
        for child, way in p.down[piece]:
            j = p.index[child]
            copies.append(remote(self.held(piece), spot, self.send.at[j], self.recv.at[j], p.near(way)))
        copies.append(remote(self.held(piece), spot, self.psend.at[i], self.precv.at[i], p.partner()))
        for copy in copies:
            copy.start()
        self.started += copies

    def across(self, piece):
        p, (h, dx, dz) = self.p, piece
        i = p.index[piece]
        spot = self.place(p.at(dx, dz, 1 - p.c), h)
        remote(spot, spot, self.psend.at[i], self.precv.at[i], p.partner()).wait_recv()

    def finish(self):
        for copy in self.started:
            copy.wait_send()


def plane_gather_kernel(x_ref, out_ref, send, recv, psend, precv, own):
    plane = Plane()
    rows, cols = x_ref.shape
    spread = Spread(plane, x_ref, out_ref, split_of(cols), send, recv, psend, precv)
    mine = pltpu.make_async_copy(
        x_ref, out_ref.at[pl.ds(pl.multiple_of(plane.expert * rows, rows), rows), :], own)
    mine.start()
    greet(plane.devices())
    for piece in plane.order:
        spread.forward(piece)
    for piece in plane.order:
        spread.across(piece)
    mine.wait()
    spread.finish()


def plane_gather(x, cid):
    rows, cols = x.shape
    n = 2 * EX * EZ
    return pl.pallas_call(
        plane_gather_kernel,
        out_shape=jax.ShapeDtypeStruct((rows * EX * EZ * CORES, cols), x.dtype),
        in_specs=[pl.BlockSpec(memory_space=pltpu.VMEM)],
        out_specs=pl.BlockSpec(memory_space=pltpu.VMEM),
        scratch_shapes=[pltpu.SemaphoreType.DMA((n,))] * 4 + [pltpu.SemaphoreType.DMA],
        compiler_params=pltpu.CompilerParams(collective_id=cid, has_side_effects=True),
        name=f"plane_gather_{cid}",
    )(x)


class Gathered:
    def __init__(self, plane, d_ref, out, rows, split, other, total, inbox, send, recv, psend, precv):
        self.p, self.d_ref, self.out, self.rows, self.split = plane, d_ref, out, rows, split
        self.other, self.total, self.inbox = other, total, inbox
        self.send, self.recv, self.psend, self.precv = send, recv, psend, precv

    def mine(self, block, h):
        start, size = self.split[h]
        rows = self.rows
        return self.d_ref.at[pl.ds(pl.multiple_of(block * rows, rows), rows), pl.ds(start, size)]

    def slot(self, ref, i, h):
        return ref.at[i, :, pl.ds(0, self.split[h][1])]

    def cross(self, piece):
        p, (h, dx, dz) = self.p, piece
        i = p.index[piece]
        return remote(self.mine(p.at(dx, dz, 1 - p.c), h), self.slot(self.other, i, h),
                      self.psend.at[i], self.precv.at[i], p.partner())

    def hop(self, piece):
        p, i = self.p, self.p.index[piece]
        return remote(self.slot(self.total, i, piece[0]), self.slot(self.inbox, i, piece[0]),
                      self.send.at[i], self.recv.at[i], p.near(BACK[p.up[piece][1]]))

    def join(self, piece):
        p, (h, dx, dz) = self.p, piece
        i = p.index[piece]
        self.cross(piece).wait_recv()
        value = self.mine(p.at(-dx, -dz, p.c), h)[...].astype(jnp.float32)
        value = value + self.slot(self.other, i, h)[...].astype(jnp.float32)
        for child, _ in p.down[piece]:
            self.hop(child).wait_recv()
            value = value + self.slot(self.inbox, p.index[child], h)[...].astype(jnp.float32)
        if piece in p.up:
            self.total[i, :, pl.ds(0, self.split[h][1])] = value.astype(self.total.dtype)
            self.hop(piece).start()
        else:
            start, size = self.split[h]
            self.out[:, pl.ds(start, size)] = value

    def finish(self):
        for piece in self.p.order:
            self.cross(piece).wait_send()
            if piece in self.p.up:
                self.hop(piece).wait_send()


def plane_reduce_kernel(d_ref, out_ref, other, total, inbox, send, recv, psend, precv):
    plane = Plane()
    rows, cols = out_ref.shape
    work = Gathered(plane, d_ref, out_ref, rows, split_of(cols), other, total, inbox,
                    send, recv, psend, precv)
    greet(plane.devices())
    for piece in plane.order[::-1]:
        work.cross(piece).start()
    for piece in plane.order[::-1]:
        work.join(piece)
    work.finish()


def reduce_scratch(rows, split, dtype):
    n = 2 * EX * EZ
    widest = max(size for _, size in split)
    return ([pltpu.VMEM((n, rows, widest), dtype)] * 3 + [pltpu.SemaphoreType.DMA((n,))] * 4)


def plane_reduce(d, cid):
    rows, cols = d.shape[0] // (EX * EZ * CORES), d.shape[1]
    return pl.pallas_call(
        plane_reduce_kernel,
        out_shape=jax.ShapeDtypeStruct((rows, cols), jnp.float32),
        in_specs=[pl.BlockSpec(memory_space=pltpu.VMEM)],
        out_specs=pl.BlockSpec(memory_space=pltpu.VMEM),
        scratch_shapes=reduce_scratch(rows, split_of(cols), d.dtype),
        compiler_params=pltpu.CompilerParams(collective_id=cid, has_side_effects=True),
        name=f"plane_reduce_{cid}",
    )(d)


def chips_by_distance():
    order, _, _ = plane_tree()
    return [(dx, dz) for h, dx, dz in order if h == 0]


def far(dx, dz):
    return abs(dx) + abs(dz)


def dispatch_kernel(x_ref, out_ref, side_ref, spread_ref, send, recv, psend, precv, csend, crecv, own):
    plane, col = Plane(), Column()
    rows, cols = x_ref.shape
    quarter = (cols - 128) // 2
    slots = out_ref.shape[0] // (EX * EZ)
    spread = Spread(plane, x_ref, spread_ref, split_of(cols), send, recv, psend, precv)
    mine = pltpu.make_async_copy(
        x_ref, spread_ref.at[pl.ds(pl.multiple_of(plane.expert * rows, rows), rows), :], own)
    mine.start()
    greet(plane.devices() + [col.near(1), col.near(-1)])
    expert = plane.expert.astype(jnp.float32)
    chips = chips_by_distance()

    def share(i, chip, source, step):
        spot = out_ref.at[pl.ds(pl.multiple_of(chip * slots, slots), slots),
                          pl.ds(pl.multiple_of(source * quarter, 128), quarter)]
        j = 2 * i + (0 if step == 1 else 1)
        return remote(spot, spot, csend.at[j], crecv.at[j], col.near(step))

    def chip_of(i):
        return plane.chip(-chips[i][0], -chips[i][1])

    shared = []

    def pick(i):
        dx, dz = chips[i]
        if i == 0:
            mine.wait()
        ox = -dx if -dx in (-1, 0, 1) else EX // 2
        oz = -dz if -(EZ // 2) < -dz <= EZ // 2 else EZ // 2
        if EX == 2:
            ox = dx
        for h in (0, 1):
            spread.across((h, ox, oz))
        chip = chip_of(i)
        both = pl.ds(pl.multiple_of(chip * CORES * rows, CORES * rows), CORES * rows)
        side = spread_ref[both, pl.ds(2 * quarter, 128)]
        side_ref[both, :] = side
        side = side.astype(jnp.float32)
        lane = lax.broadcasted_iota(jnp.int32, side.shape, 1)
        place = pltpu.roll(side, 128 - 8, 1)
        place = jnp.sum(jnp.where((side == expert) & (lane < 8), place, 0.0), axis=1, keepdims=True)
        token = lax.broadcasted_iota(jnp.int32, (CORES * rows, slots), 0)
        slot = lax.broadcasted_iota(jnp.int32, (CORES * rows, slots), 1)
        per = slots // CORES
        wanted = jnp.where(token // rows == slot // per, slot % per + 1, 0).astype(jnp.float32)
        pickers = jnp.where((wanted == place) & (wanted > 0.0), 1.0, 0.0).astype(jnp.bfloat16)

        def chosen(start):
            return lax.dot_general(
                pickers, spread_ref[both, pl.ds(start, quarter)], (((0,), (0,)), ((), ())),
                preferred_element_type=jnp.float32).astype(out_ref.dtype)

        here = pl.ds(pl.multiple_of(chip * slots, slots), slots)
        out_ref[here, pl.ds(pl.multiple_of(col.y * quarter, 128), quarter)] = chosen(quarter)
        for step in (1, -1):
            copy = share(i, chip, col.y, step)
            copy.start()
            shared.append(copy)
        out_ref[here, pl.ds(pl.multiple_of(col.at(2) * quarter, 128), quarter)] = chosen(0)

    done = 0
    for piece in plane.order:
        spread.forward(piece)
        if done < len(chips) and far(*chips[done]) < far(*piece[1:]):
            pick(done)
            done += 1
    while done < len(chips):
        pick(done)
        done += 1
    for i in range(len(chips)):
        for step in (1, -1):
            share(i, chip_of(i), col.at(-step), step).wait_recv()
    for copy in shared:
        copy.wait_send()
    spread.finish()


def dispatch(x, slots, cid):
    rows, cols = x.shape
    n = 2 * EX * EZ
    blocks = EX * EZ * CORES
    return pl.pallas_call(
        dispatch_kernel,
        out_shape=(jax.ShapeDtypeStruct((slots, (cols - 128) // 2 * HALVES), x.dtype),
                   jax.ShapeDtypeStruct((rows * blocks, 128), x.dtype)),
        in_specs=[pl.BlockSpec(memory_space=pltpu.VMEM)],
        out_specs=[pl.BlockSpec(memory_space=pltpu.VMEM)] * 2,
        scratch_shapes=[pltpu.VMEM((rows * blocks, cols), x.dtype)]
        + [pltpu.SemaphoreType.DMA((n,))] * 6 + [pltpu.SemaphoreType.DMA],
        compiler_params=pltpu.CompilerParams(collective_id=cid, has_side_effects=True),
        name=f"dispatch_{cid}",
    )(x)


def give_back_kernel(r_ref, pick_ref, out_ref, dense, cin, sums, last, opposite, other, total, inbox,
                     send, recv, psend, precv, csend, crecv, lsem):
    plane, col = Plane(), Column()
    rows, quarter = out_ref.shape
    slots = r_ref.shape[0] // (EX * EZ)
    split = ((0, quarter), (quarter, quarter))
    work = Gathered(plane, dense, sums, rows, split, other, total, inbox, send, recv, psend, precv)
    greet(plane.devices() + [col.near(1), col.near(-1), col.near(2)])
    chips = chips_by_distance()

    def chip_of(i):
        return plane.chip(-chips[i][0], -chips[i][1])

    def rows_of(i, y):
        return r_ref.at[pl.ds(pl.multiple_of(chip_of(i) * slots, slots), slots),
                        pl.ds(pl.multiple_of(y * quarter, 128), quarter)]

    def share(i, step):
        j = 2 * i + (0 if step == 1 else 1)
        return remote(rows_of(i, col.at(step)), cin.at[j], csend.at[j], crecv.at[j], col.near(step))

    def lay_out(i, h):
        if h == 0:
            value = rows_of(i, col.at(2))[...]
        else:
            value = rows_of(i, col.y)[...].astype(jnp.float32)
            for step in (1, -1):
                share(i, step).wait_recv()
                value = value + cin[2 * i + (0 if step == 1 else 1)].astype(jnp.float32)
            value = value.astype(r_ref.dtype)
        chip = chip_of(i)
        both = pl.ds(pl.multiple_of(chip * CORES * rows, CORES * rows), CORES * rows)
        dense[both, pl.ds(h * quarter, quarter)] = jnp.dot(
            pick_ref[both, :], value, preferred_element_type=jnp.float32).astype(dense.dtype)
        dx, dz = chips[i]
        ox = -dx if -dx in (-1, 0, 1) else EX // 2
        oz = -dz if -(EZ // 2) < -dz <= EZ // 2 else EZ // 2
        if EX == 2:
            ox = dx
        work.cross((h, ox, oz)).start()

    backward = list(range(len(chips)))[::-1]
    for i in backward:
        for step in (1, -1):
            share(i, step).start()
    most = max(far(*c) for c in chips)
    by_level = [[i for i in backward if far(*chips[i]) == level] for level in range(most + 1)]
    for level in range(most, -2, -1):
        for h in (0, 1):
            if level >= 0:
                for i in by_level[level]:
                    lay_out(i, h)
            if level < most:
                for i in by_level[level + 1]:
                    work.join((h,) + chips[i])
    last[...] = sums[:, pl.ds(0, quarter)].astype(last.dtype)
    final = remote(last, opposite, lsem.at[0], lsem.at[1], col.near(2))
    final.start()
    final.wait_recv()
    value = sums[:, pl.ds(quarter, quarter)] + opposite[...].astype(jnp.float32)
    out_ref[...] = value.astype(out_ref.dtype)
    final.wait_send()
    for i in range(len(chips)):
        for step in (1, -1):
            share(i, step).wait_send()
    work.finish()


def give_back(r, pickers, cid):
    quarter = r.shape[1] // HALVES
    rows = pickers.shape[0] // (EX * EZ * CORES)
    n = 2 * EX * EZ
    slots = r.shape[0] // (EX * EZ)
    split = ((0, quarter), (quarter, quarter))
    return pl.pallas_call(
        give_back_kernel,
        out_shape=jax.ShapeDtypeStruct((rows, quarter), r.dtype),
        in_specs=[pl.BlockSpec(memory_space=pltpu.VMEM)] * 2,
        out_specs=pl.BlockSpec(memory_space=pltpu.VMEM),
        scratch_shapes=[pltpu.VMEM((pickers.shape[0], 2 * quarter), r.dtype),
                        pltpu.VMEM((n, slots, quarter), r.dtype),
                        pltpu.VMEM((rows, 2 * quarter), jnp.float32),
                        pltpu.VMEM((rows, quarter), r.dtype),
                        pltpu.VMEM((rows, quarter), r.dtype)]
        + reduce_scratch(rows, split, r.dtype)
        + [pltpu.SemaphoreType.DMA((n,))] * 2 + [pltpu.SemaphoreType.DMA((2,))],
        compiler_params=pltpu.CompilerParams(collective_id=cid, has_side_effects=True),
        name=f"give_back_{cid}",
    )(r, pickers)


class Column:
    def __init__(self):
        self.y = lax.axis_index("half")

    def at(self, step):
        return ring(self.y, step, HALVES)

    def near(self, step):
        return {"half": self.at(step)}


NEAR = [(0, 1), (1, -1), (1, 1), (0, -1)]


def column_gather_kernel(x_ref, out_ref, send, recv, own):
    col = Column()
    rows, cols = x_ref.shape
    part = rows // 2
    greet([col.near(1), col.near(-1)])

    def place(source, h):
        return out_ref.at[pl.ds(h * part, part), pl.ds(pl.multiple_of(source * cols, 128), cols)]

    def copy(i, src, source, h, step):
        return pltpu.make_async_remote_copy(
            src_ref=src, dst_ref=place(source, h), send_sem=send.at[i], recv_sem=recv.at[i],
            device_id=col.near(step), device_id_type=MESH)

    started = []
    for i, (h, step) in enumerate(NEAR):
        started.append(copy(i, x_ref.at[pl.ds(h * part, part), :], col.y, h, step))
    mine = pltpu.make_async_copy(
        x_ref, out_ref.at[:, pl.ds(pl.multiple_of(col.y * cols, 128), cols)], own)
    for c in started:
        c.start()
    mine.start()
    for i, (h, step) in enumerate(NEAR):
        source = col.at(-step)
        copy(i, place(source, h), source, h, step).wait_recv()
        if i < 2:
            c = copy(4 + i, place(source, h), source, h, step)
            c.start()
            started.append(c)
    for i, (h, step) in enumerate(NEAR[:2]):
        source = col.at(2)
        copy(4 + i, place(source, h), source, h, step).wait_recv()
    mine.wait()
    for c in started:
        c.wait_send()


def column_gather(x, cid):
    rows, cols = x.shape
    return pl.pallas_call(
        column_gather_kernel,
        out_shape=jax.ShapeDtypeStruct((rows, cols * HALVES), x.dtype),
        in_specs=[pl.BlockSpec(memory_space=pltpu.VMEM)],
        out_specs=pl.BlockSpec(memory_space=pltpu.VMEM),
        scratch_shapes=[pltpu.SemaphoreType.DMA((6,))] * 2 + [pltpu.SemaphoreType.DMA],
        compiler_params=pltpu.CompilerParams(collective_id=cid, has_side_effects=True),
        name=f"column_gather_{cid}",
    )(x)


def column_reduce_kernel(d_ref, out_ref, inbox, total, send, recv):
    col = Column()
    rows, cols = out_ref.shape
    part = rows // 2
    tile = 32
    greet([col.near(1), col.near(-1)])

    def mine(dest, start, size):
        return d_ref.at[pl.ds(start, size), pl.ds(pl.multiple_of(dest * cols, 128), cols)]

    def copy(i, src, step):
        return pltpu.make_async_remote_copy(
            src_ref=src, dst_ref=inbox.at[i], send_sem=send.at[i], recv_sem=recv.at[i],
            device_id=col.near(step), device_id_type=MESH)

    started = []
    for i, (h, step) in enumerate(NEAR[:2]):
        started.append(copy(4 + i, mine(col.at(2), h * part, part), -step))
    for i, (h, step) in enumerate(NEAR[2:]):
        started.append(copy(2 + i, mine(col.at(-step), h * part, part), -step))
    for c in started:
        c.start()
    for i, (h, step) in enumerate(NEAR[:2]):
        copy(4 + i, total.at[i], step).wait_recv()

        def join(t, carry, i=i, h=h, step=step):
            start = pl.multiple_of(t * tile, tile)
            a = mine(col.at(-step), pl.multiple_of(h * part + start, tile), tile)[...]
            b = inbox[4 + i, pl.ds(start, tile), :]
            total[i, pl.ds(start, tile), :] = (
                a.astype(jnp.float32) + b.astype(jnp.float32)).astype(total.dtype)
            return carry

        lax.fori_loop(0, part // tile, join, 0)
        c = copy(i, total.at[i], -step)
        c.start()
        started.append(c)
    for i in (2, 3, 0, 1):
        copy(i, total.at[0], 1).wait_recv()
    for h in (0, 1):
        a, b = [i for i in range(4) if NEAR[i][0] == h]

        def join(t, carry, a=a, b=b, h=h):
            start = pl.multiple_of(t * tile, tile)
            spot = pl.multiple_of(h * part + start, tile)
            value = mine(col.y, spot, tile)[...].astype(jnp.float32)
            value = value + inbox[a, pl.ds(start, tile), :].astype(jnp.float32)
            value = value + inbox[b, pl.ds(start, tile), :].astype(jnp.float32)
            out_ref[pl.ds(spot, tile), :] = value.astype(out_ref.dtype)
            return carry

        lax.fori_loop(0, part // tile, join, 0)
    for c in started:
        c.wait_send()


def column_reduce(d, cid, dtype):
    rows, cols = d.shape[0], d.shape[1] // HALVES
    return pl.pallas_call(
        column_reduce_kernel,
        out_shape=jax.ShapeDtypeStruct((rows, cols), dtype),
        in_specs=[pl.BlockSpec(memory_space=pltpu.VMEM)],
        out_specs=pl.BlockSpec(memory_space=pltpu.VMEM),
        scratch_shapes=[pltpu.VMEM((6, rows // 2, cols), d.dtype),
                        pltpu.VMEM((2, rows // 2, cols), d.dtype)]
        + [pltpu.SemaphoreType.DMA((6,))] * 2,
        compiler_params=pltpu.CompilerParams(collective_id=cid, has_side_effects=True),
        name=f"column_reduce_{cid}",
    )(d)


def dequant(code_vals, low_edge, high_edge):
    groups = low_edge.shape[0]
    scaled = code_vals.astype(jnp.float32).reshape(groups, -1, code_vals.shape[-1]) / 255.0
    weight = low_edge[:, None, :] + (high_edge - low_edge)[:, None, :] * scaled
    return weight.reshape(code_vals.shape).astype(jnp.bfloat16)


def range_grads(grad_weight, code_vals, groups):
    shaped = grad_weight.reshape(groups, -1, grad_weight.shape[-1])
    scaled = code_vals.astype(jnp.float32).reshape(groups, -1, code_vals.shape[-1]) / 255.0
    low_grad = jnp.sum(shaped * (1.0 - scaled), axis=1)
    high_grad = jnp.sum(shaped * scaled, axis=1)
    return (low_grad, high_grad)


def contract_rows(left, right):
    return lax.dot_general(
        left, right, (((0,), (0,)), ((), ())), preferred_element_type=jnp.float32
    )


def contract_cols(left, right):
    return lax.dot_general(
        left, right, (((1,), (1,)), ((), ())), preferred_element_type=jnp.float32
    )


def local(
    tokens, target, routes, route_scores, in_codes, in_low, in_high, down_codes, down_low, down_high
):
    bf16, f32 = jnp.bfloat16, jnp.float32
    experts = lax.axis_size("expert")
    expert = lax.axis_index("expert")
    tok_count, top_count = routes.shape
    quarter = target.shape[1]
    all_tokens = experts * tok_count
    slots = experts * min(tok_count, 2 * tok_count * top_count // experts)

    weights = route_scores / jnp.sum(route_scores, axis=1, keepdims=True)
    same = routes[:, :, None, None] == routes[None, None, :, :]
    earlier = jnp.arange(tok_count)[:, None] > jnp.arange(tok_count)[None, :]
    place = jnp.sum((same & earlier[:, None, :, None]).astype(f32), axis=(2, 3)) + 1.0
    terms, rest = [routes.astype(bf16), place.astype(bf16)], weights
    for _ in range(3):
        term = lax.reduce_precision(rest, 8, 7)
        terms.append(term.astype(bf16))
        rest = rest - term
    side = jnp.concatenate(terms, axis=1)
    side = jnp.pad(side, ((0, 0), (0, 128 - side.shape[1])))
    half = lax.axis_index("half")
    own = lax.dynamic_slice_in_dim(tokens, half * quarter, quarter, 1)
    opposite = lax.dynamic_slice_in_dim(tokens, (half + 2) % HALVES * quarter, quarter, 1)
    expert_rows, side = dispatch(jnp.concatenate([opposite, own, side], axis=1), slots, 0)

    side = side[:, :5 * top_count].astype(f32)
    named = side[:, :top_count] == expert.astype(f32)
    weight_of = sum(side[:, k * top_count:(k + 1) * top_count] for k in (2, 3, 4))
    weight_of = jnp.sum(jnp.where(named, weight_of, 0.0), axis=1)
    place = jnp.sum(jnp.where(named, side[:, top_count:2 * top_count], 0.0), axis=1).astype(jnp.int32)
    per = slots // experts
    block = jnp.arange(all_tokens, dtype=jnp.int32) // tok_count
    slot_of = jnp.where(place > 0, block * per + place - 1, -1)
    picks = slot_of[None, :] == jnp.arange(slots, dtype=jnp.int32)[:, None]
    slot_weight = jnp.sum(jnp.where(picks, weight_of[None, :], 0.0), axis=1)
    picks = picks.astype(bf16)
    in_chip = jnp.where(place > 0, block % CORES * per + place - 1, -1)
    chip_picks = (in_chip[:, None] == jnp.arange(CORES * per, dtype=jnp.int32)[None, :]).astype(bf16)

    w_gate = dequant(in_codes[0, 0], in_low[0, 0], in_high[0, 0])
    w_up = dequant(in_codes[0, 1], in_low[0, 1], in_high[0, 1])
    w_down = dequant(down_codes[0], down_low[0], down_high[0])

    gate_pre = jnp.dot(expert_rows, w_gate, preferred_element_type=f32)
    up_pre = jnp.dot(expert_rows, w_up, preferred_element_type=f32)
    sigmoid_gate = jax.nn.sigmoid(gate_pre)
    gate_act = gate_pre * sigmoid_gate
    hidden = (gate_act * up_pre).astype(bf16)
    hidden_all = column_gather(hidden, 2)
    out_rows = jnp.dot(hidden_all, w_down, preferred_element_type=f32)
    out_rows = (out_rows * slot_weight[:, None]).astype(bf16)
    mixed_out = plane_reduce(contract_rows(picks, out_rows).astype(bf16), 3)
    recon_error = mixed_out - target.astype(f32)
    errors = plane_gather(recon_error.astype(bf16), 4)
    error_grads = jnp.dot(picks, errors, preferred_element_type=f32)
    error_grads = (error_grads * slot_weight[:, None]).astype(bf16)
    partial_hidden = contract_cols(error_grads, w_down).astype(bf16)
    grad_hidden = column_reduce(partial_hidden, 5, f32)
    grad_gate = (
        grad_hidden * up_pre * sigmoid_gate * (1.0 + gate_pre * (1.0 - sigmoid_gate))
    ).astype(bf16)
    grad_up = (grad_hidden * gate_act).astype(bf16)
    row_part = (contract_cols(grad_gate, w_gate) + contract_cols(grad_up, w_up)).astype(bf16)
    grad_tokens = give_back(row_part, chip_picks, 6)

    groups_width = in_low.shape[2]
    gate_low, gate_high = range_grads(
        contract_rows(expert_rows, grad_gate), in_codes[0, 0], groups_width
    )
    up_low, up_high = range_grads(contract_rows(expert_rows, grad_up), in_codes[0, 1], groups_width)
    down_lowg, down_highg = range_grads(
        contract_rows(hidden_all, error_grads), down_codes[0], down_low.shape[1]
    )
    in_grad = jnp.stack([gate_low, gate_high, up_low, up_high])[None]
    down_grad = jnp.stack([down_lowg, down_highg])[None]
    return (grad_tokens, in_grad, down_grad)


def solution(mesh):
    placed = (
        P("expert", None),
        P("expert", "half"),
        P("expert", None),
        P("expert", None),
        P("expert", None, None, "half"),
        P("expert", None, None, "half"),
        P("expert", None, None, "half"),
        P("expert", None, "half"),
        P("expert", None, "half"),
        P("expert", None, "half"),
    )
    return jax.shard_map(
        local,
        mesh=mesh,
        in_specs=placed,
        out_specs=(
            P("expert", "half"),
            P("expert", None, None, "half"),
            P("expert", None, None, "half"),
        ),
        check_vma=False,
    )
```
